32 devices in a mesh: groups: 2 (over y), blk: 16 (over z, x, core).
Axes of the slice: x: 2, y: 2, z: 4, core: 2. Of those that a mesh axis runs over, the one named last changes fastest.
Arguments:
- query_hidden: bfloat16 [512, 32, 768], P(('groups', 'blk')), parts along dimension 0, may hold values from -6 to 6
- passage_hidden: bfloat16 [256, 180, 768], P(('groups', 'blk')), parts along dimension 0, may hold values from -6 to 6
- projection: bfloat16 [768, 128], replicated, may hold values from -0.21875 to 0.21875
- teacher_rows: float32 [512, 32], P(('groups', 'blk')), parts along dimension 0, may hold values from -12 to 12
- teacher_pos: int32 [512], P(('groups', 'blk')), parts along dimension 0, may hold values from 0 to 255, each once
- neg_count: int32 [512], P(('groups', 'blk')), parts along dimension 0, may hold values from 8 to 32
- pass_len: int32 [256], P(('groups', 'blk')), parts along dimension 0, may hold values from 19 to 180
Outputs:
- loss: float32 [512], P(('groups', 'blk')), parts along dimension 0
- grad_w: float32 [1536, 128], P(('groups', 'blk')), parts along dimension 0
The draws below stay inside these ranges and needn't reach their ends.
There are 2 independent parts, one for each index of `groups`. The reference program is written for one: setup_inputs(seed, part) draws one part's arguments, and reference() takes and returns one part's arrays. A program takes and returns all parts, laid end to end along the dimension named above; an argument that names none is the same for every part. Nothing has to cross between parts.
Inputs may be any that keep to these rules, and one draw needn't show every extreme that they name: A permutation: the teacher scores of query q are stored as row teacher_pos[q] of teacher_rows.
All inputs are finite; a program needn't handle non-finite values.
Results may differ from the reference program's by a relative error of at most 0.0073.
Values may be sent and summed in bfloat16 or wider, within the bound.
A program may use at most 128 MiB of HBM per device.

```python
import jax
import jax.numpy as jnp
from jax import lax

H = 768
DIM = 128
QT = 32
PT = 180
CYCLE = 4
Q_DEV = 16
P_DEV = 8
CAND = 32
NQ = 256
NP = 128
N_BLK = 16


def draw_neg_count(key, part):
    counts = jax.random.randint(key, (NQ,), P_DEV, CAND + 1, dtype=jnp.int32)
    return counts.at[0].set(CAND).at[1].set(P_DEV)


def draw_pass_len(key, part):
    lowest = PT // 10 + 1
    lengths = jax.random.randint(key, (NP,), lowest, PT + 1, dtype=jnp.int32)
    return lengths.at[0].set(PT).at[1].set(lowest)


def raised(entries, key, source, target, shards_of, factor):
    def block_of(axis_at):
        return (jnp.arange(entries.shape[axis_at]) // (entries.shape[axis_at] // shards_of)).reshape((-1,) + (1,) * (entries.ndim - 1 - axis_at))

    first = jax.random.permutation(key, shards_of)[block_of(target)]
    other_side = (block_of(target) + shards_of // 2) % shards_of
    return jnp.where((block_of(source) == first) | (block_of(source) == other_side), factor * entries, entries)


def levels(rng, extent, cuts, least, largest):
    factor_of, own = 1.0, jax.random.fold_in(rng, 6)
    for dim, parts in cuts:
        draws = jnp.exp(jax.random.uniform(jax.random.fold_in(own, dim), (parts,), jnp.float32, least / len(cuts), largest / len(cuts)))
        factor_of = factor_of * jnp.repeat(draws, extent[dim] // parts).reshape([-1 if axis == dim else 1 for axis in range(len(extent))])
    return factor_of


def bell_draw(rng, dims, deviation, reach, shards=(), kind=jnp.bfloat16):
    level = levels(rng, dims, shards, -0.22, 0.18) if shards else 1.0
    values = jax.random.normal(rng, dims, jnp.float32) * deviation * level
    return jnp.minimum(jnp.maximum(values, -reach), reach).astype(kind)


def noise_with(key, shape, spread, reach, split, heavy, held_as=jnp.bfloat16):
    drawn = spread * jax.random.normal(key, shape, jnp.float32)
    if split:
        drawn = drawn * levels(key, shape, split, -0.22, 0.18)
    return jnp.clip(raised(drawn, jax.random.fold_in(key, 3), *heavy), -reach, reach).astype(held_as)


def setup_inputs(seed: int = 0, part: int = 0) -> dict:
    key_list = jax.random.split(jax.random.key(seed), 8)
    own_keys = jax.random.split(jax.random.fold_in(key_list[7], part), 8)
    return {
        "query_hidden": noise_with(own_keys[0], (NQ, QT, H), 1.0, 6.0, ((0, 16),), (0, 2, 16, 2.0)),
        "passage_hidden": noise_with(own_keys[1], (NP, PT, H), 1.0, 6.0, ((0, 16),), (0, 2, 16, 2.0)),
        "projection": bell_draw(key_list[2], (H, DIM), H ** -0.5, 0.21875),
        "teacher_rows": bell_draw(own_keys[3], (NQ, CAND), 3.0, 12.0, ((0, 16),), jnp.float32),
        "teacher_pos": jax.random.permutation(own_keys[4], NQ).astype(jnp.int32),
        "neg_count": draw_neg_count(jax.random.fold_in(jax.random.fold_in(key_list[7], part), 71), part),
        "pass_len": draw_pass_len(jax.random.fold_in(jax.random.fold_in(key_list[7], part), 71), part),
    }


smoothing_heat_factor = 0.05
epsilon = 1e-06

def normalize(raw):
    length = jnp.sqrt(lax.optimization_barrier(jnp.sum(raw * raw, axis=1, keepdims=True)) + epsilon)
    return (raw / length, length)

def token_terms(query_flat, passage_flat, lengths):
    count = lengths.shape[0]
    token_affinity_table = lax.dot_general(query_flat, passage_flat, (((1,), (1,)), ((), ())), preferred_element_type=jnp.float32)
    token_affinity_table = token_affinity_table.reshape(query_flat.shape[0], count, -1)
    pairwise_dot_entries = jnp.arange(token_affinity_table.shape[2], dtype=jnp.int32)[None, :] < lengths[:, None]
    natural_power_entries = jnp.where(pairwise_dot_entries[None], jnp.exp(token_affinity_table / smoothing_heat_factor), 0.0)
    return (natural_power_entries, lax.optimization_barrier(jnp.sum(natural_power_entries, axis=2)))

def soft_scores(query_flat, passage_flat, lengths, query_matrix):
    natural_power_entries, power_totals_row = token_terms(query_flat, passage_flat, lengths)
    smooth_peak_values = smoothing_heat_factor * jnp.log(power_totals_row)
    return lax.optimization_barrier(jnp.sum(smooth_peak_values.reshape(query_matrix, -1, lengths.shape[0]), axis=1))

def score_grads(query_flat, passage_flat, lengths, score_grad):
    natural_power_entries, power_totals_row = token_terms(query_flat, passage_flat, lengths)
    rows = query_flat.shape[0]
    query_matrix, count = score_grad.shape
    scale = (score_grad[:, None, :] / power_totals_row.reshape(query_matrix, -1, count)).reshape(rows, count)
    weights = (natural_power_entries * scale[:, :, None]).reshape(rows, -1).astype(jnp.bfloat16)
    query_grad = jnp.dot(weights, passage_flat, preferred_element_type=jnp.float32)
    passage_grad = lax.dot_general(weights, query_flat, (((0,), (0,)), ((), ())), preferred_element_type=jnp.float32)
    return (query_grad, passage_grad)

def kl_terms(student, teacher, counts):
    valid = jnp.arange(student.shape[1], dtype=jnp.int32)[None, :] < counts[:, None]
    student_exp = jnp.where(valid, jnp.exp(student), 0.0)
    student_total = lax.optimization_barrier(jnp.sum(student_exp, axis=1, keepdims=True))
    teacher_exp = jnp.where(valid, jnp.exp(teacher), 0.0)
    teacher_total = lax.optimization_barrier(jnp.sum(teacher_exp, axis=1, keepdims=True))
    student_prob = student_exp / student_total
    teacher_prob = teacher_exp / teacher_total
    gap = teacher - jnp.log(teacher_total) - (student - jnp.log(student_total))
    loss = lax.optimization_barrier(jnp.sum(jnp.where(valid, teacher_prob * gap, 0.0), axis=1))
    return (loss, student_prob - teacher_prob)

def raw_grad(unit, length, grad):
    return ((grad - unit * lax.optimization_barrier(jnp.sum(unit * grad, axis=1, keepdims=True))) / length).astype(jnp.bfloat16)

def block_scores(items):
    return soft_scores(items[0], items[1], items[2], Q_DEV)

def block_grads(items):
    return score_grads(items[0], items[1], items[2], items[3])

def reference(query_hidden, passage_hidden, projection, teacher_rows, teacher_pos, neg_count, pass_len):
    query_flat = query_hidden.reshape(NQ * QT, H)
    passage_flat = passage_hidden.reshape(NP * PT, H)
    query_unit, query_length = normalize(jnp.dot(query_flat, projection, preferred_element_type=jnp.float32))
    passage_unit, passage_length = normalize(jnp.dot(passage_flat, projection, preferred_element_type=jnp.float32))
    query_blocks = query_unit.astype(jnp.bfloat16).reshape(N_BLK, Q_DEV * QT, DIM)
    passage_blocks = passage_unit.astype(jnp.bfloat16).reshape(N_BLK, P_DEV * PT, DIM)
    length_blocks = pass_len.reshape(N_BLK, P_DEV)
    teacher = jnp.take(teacher_rows, teacher_pos, axis=0)
    score_parts = []
    for offset in range(CYCLE):
        moved = jnp.roll(passage_blocks, -offset, axis=0)
        moved_len = jnp.roll(length_blocks, -offset, axis=0)
        score_parts.append(lax.map(block_scores, (query_blocks, moved, moved_len)))
    student = jnp.concatenate(score_parts, axis=2).reshape(NQ, CAND)
    loss, score_grad = kl_terms(student, teacher, neg_count)
    grad_blocks = score_grad.reshape(N_BLK, Q_DEV, CAND)
    query_total = jnp.zeros((N_BLK, Q_DEV * QT, DIM), jnp.float32)
    passage_total = jnp.zeros((N_BLK, P_DEV * PT, DIM), jnp.float32)
    for offset in range(CYCLE):
        moved = jnp.roll(passage_blocks, -offset, axis=0)
        moved_len = jnp.roll(length_blocks, -offset, axis=0)
        portion_derivative = grad_blocks[:, :, offset * P_DEV:(offset + 1) * P_DEV]
        query_part, passage_part = lax.map(block_grads, (query_blocks, moved, moved_len, portion_derivative))
        query_total = query_total + query_part
        passage_total = passage_total + jnp.roll(passage_part, offset, axis=0)
    query_raw = raw_grad(query_unit, query_length, query_total.reshape(NQ * QT, DIM))
    document_unprojected = raw_grad(passage_unit, passage_length, passage_total.reshape(NP * PT, DIM))
    contract = (((0,), (0,)), ((), ()))
    grad_w = lax.dot_general(query_flat, query_raw, contract, preferred_element_type=jnp.float32)
    grad_w = grad_w + lax.dot_general(passage_flat, document_unprojected, contract, preferred_element_type=jnp.float32)
    return (loss, grad_w)
```

```python
import functools
import math

import jax
import jax.numpy as jnp
from jax import lax
from jax.experimental import pallas as pl
from jax.experimental.pallas import tpu as pltpu
from jax.sharding import PartitionSpec as P

CYCLE = 4
HEAT = 0.05
EPSILON = 1e-06
EXP2_SCALE = math.log2(math.e) / HEAT
NT = (((1,), (1,)), ((), ()))
TN = (((0,), (0,)), ((), ()))


def dot32(a, b, dims):
    return lax.dot_general(
        a, b, dims, precision=lax.Precision.HIGHEST, preferred_element_type=jnp.float32
    )


def kernel(
    n, link_dtype,
    qh_ref, ph_ref, proj_ref, rows_ref, pos_ref, cnt_ref, len_ref,
    loss_ref, grad_ref,
    teach_own, teach_all, qraw, q_all, pv, plen, pu, exps, den, w_buf, pgrad,
    s_send, s_recv, g_send, g_recv, qg_send, qg_recv, part, part_own, part_recv,
    teach_ss, teach_rs, q_ss, q_rs, s_ss, s_rs, g_ss, g_rs, qg_ss, qg_rs, part_ss, part_rs,
):
    me = lax.axis_index("blk")
    queries, q_tokens, width = qh_ref.shape
    passages, p_tokens, _ = ph_ref.shape
    dim = proj_ref.shape[1]
    q_rows = queries * q_tokens
    padded = pu.shape[0] // passages

    def peer(shift):
        return lax.rem(me + shift + n, n)

    def remote(src, dst, ss, rs, target):
        return pltpu.make_async_remote_copy(
            src_ref=src, dst_ref=dst, send_sem=ss, recv_sem=rs,
            device_id={"blk": target}, device_id_type=pl.DeviceIdType.MESH,
        )

    barrier = pltpu.get_barrier_semaphore()

    @pl.loop(1, n)
    def _(k):
        pl.semaphore_signal(
            barrier, inc=1, device_id={"blk": peer(k)}, device_id_type=pl.DeviceIdType.MESH
        )

    projection = proj_ref[...]
    q_hidden = qh_ref[...].reshape(q_rows, width)
    raw = jnp.dot(q_hidden, projection, preferred_element_type=jnp.float32)
    qraw[...] = raw
    q_len = jnp.sqrt(jnp.sum(raw * raw, axis=1, keepdims=True) + EPSILON)
    q_all[0] = (raw / q_len).astype(jnp.bfloat16)
    teach_own[...] = jnp.zeros(teach_own.shape, jnp.float32)
    teach_own[:, : rows_ref.shape[1]] = rows_ref[...]
    teach_all[me] = teach_own[...]
    pl.semaphore_wait(barrier, n - 1)

    def q_copy(o):
        return remote(q_all.at[0], q_all.at[o], q_ss.at[o], q_rs.at[o], peer(o))

    for o in range(1, CYCLE):
        q_copy(o).start()

    def teach_send(k):
        return remote(teach_own, teach_all.at[me], teach_ss.at[k], teach_rs.at[k], peer(k))

    def teach_recv(k):
        return remote(teach_own, teach_all.at[peer(-k)], teach_ss.at[k], teach_rs.at[k], peer(k))

    @pl.loop(1, n)
    def _(k):
        teach_send(k).start()

    pv[...] = jnp.zeros(pv.shape, jnp.float32)
    plen[...] = jnp.ones(plen.shape, jnp.float32)

    for p in range(passages):
        at = p * padded
        raw_p = jnp.dot(ph_ref[p], projection, preferred_element_type=jnp.float32)
        length = jnp.sqrt(jnp.sum(raw_p * raw_p, axis=1, keepdims=True) + EPSILON)
        pv[at : at + p_tokens] = raw_p / length
        plen[at : at + p_tokens] = jnp.broadcast_to(length, raw_p.shape)
    pu[...] = pv[...].astype(jnp.bfloat16)
    pgrad[...] = jnp.zeros(pgrad.shape, jnp.float32)

    low = lax.broadcasted_iota(jnp.int32, (queries, q_rows), 0) * q_tokens
    lane = lax.broadcasted_iota(jnp.int32, (queries, q_rows), 1)
    spread = jnp.where((lane >= low) & (lane < low + q_tokens), 1.0, 0.0)
    token = lax.broadcasted_iota(jnp.int32, (padded, q_rows), 0)

    s_send[...] = jnp.zeros(s_send.shape, jnp.float32)
    g_send[...] = jnp.zeros(g_send.shape, jnp.float32)

    def s_copy(o):
        return remote(s_send.at[o], s_recv.at[o], s_ss.at[o], s_rs.at[o], peer(-o))

    def g_copy(o):
        return remote(g_send.at[o], g_recv.at[o], g_ss.at[o], g_rs.at[o], peer(o))

    def qg_copy(o):
        return remote(qg_send.at[o], qg_recv.at[o], qg_ss.at[o], qg_rs.at[o], peer(-o))

    def score(o):
        units = q_all[o]

        @pl.loop(0, passages)
        def _(p):
            at = pl.ds(pl.multiple_of(p * padded, padded), padded)
            sims = lax.dot_general(pu[at], units, NT, preferred_element_type=jnp.float32)
            e = jnp.where(token < len_ref[0, p], jnp.exp2(sims * EXP2_SCALE), 0.0)
            exps[o, at] = e
            den[o, pl.ds(p, 1)] = jnp.sum(e, axis=0, keepdims=True)

        peaks = HEAT * jnp.log(den[o])
        return dot32(peaks, spread, NT)

    own_scores = score(0)
    for o in range(1, CYCLE):
        q_copy(o).wait_recv()
        s_send[o, :, :queries] = score(o)
        s_copy(o).start()

    @pl.loop(1, n)
    def _(k):
        teach_recv(k).wait_recv()

    stored = teach_all[...].reshape(n * queries, teach_all.shape[2])
    cand = CYCLE * passages
    rows = lax.broadcasted_iota(jnp.int32, (n * queries, queries), 0)
    pick = jnp.where(rows == pos_ref[...], 1.0, 0.0)
    teacher = dot32(jnp.transpose(stored)[:cand], pick, (((1,), (0,)), ((), ())))
    valid = lax.broadcasted_iota(jnp.int32, (cand, queries), 0) < cnt_ref[...]
    teacher_exp = jnp.where(valid, jnp.exp(teacher), 0.0)
    teacher_total = jnp.sum(teacher_exp, axis=0, keepdims=True)
    teacher_prob = teacher_exp / teacher_total
    teacher_log = teacher - jnp.log(teacher_total)

    student_parts = [own_scores]
    for o in range(1, CYCLE):
        s_copy(o).wait_recv()
        student_parts.append(s_recv[o, :, :queries])
    student = jnp.concatenate(student_parts, axis=0)
    student_exp = jnp.where(valid, jnp.exp(student), 0.0)
    student_total = jnp.sum(student_exp, axis=0, keepdims=True)
    score_grad = student_exp / student_total - teacher_prob
    for o in range(1, CYCLE):
        g_send[o, :, :queries] = score_grad[o * passages : (o + 1) * passages]
        g_copy(o).start()
    gap = teacher_log - (student - jnp.log(student_total))
    loss_ref[...] = jnp.sum(jnp.where(valid, teacher_prob * gap, 0.0), axis=0, keepdims=True)

    def backward(o, grads):
        units = q_all[o]
        den[o] = dot32(grads, spread, (((1,), (0,)), ((), ()))) / den[o]

        @pl.loop(0, passages)
        def _(p):
            at = pl.ds(pl.multiple_of(p * padded, padded), padded)
            w = (exps[o, at] * den[o, pl.ds(p, 1)]).astype(jnp.bfloat16)
            w_buf[at] = w
            pgrad[at] += jnp.dot(w, units, preferred_element_type=jnp.float32)

        return lax.dot_general(pu[...], w_buf[...], TN, preferred_element_type=jnp.float32)

    q_total = backward(0, score_grad[:passages])
    for o in range(1, CYCLE):
        g_copy(o).wait_recv()
        qg_send[o] = backward(o, g_recv[o, :, :queries]).astype(link_dtype)
        qg_copy(o).start()

    term = jnp.zeros((dim, width), jnp.float32)
    for p in range(passages):
        at = p * padded
        v = pv[at : at + p_tokens]
        g = pgrad[at : at + p_tokens]
        raw_g = (g - v * jnp.sum(v * g, axis=1, keepdims=True)) / plen[at : at + p_tokens]
        term = term + lax.dot_general(
            raw_g.astype(jnp.bfloat16), ph_ref[p], TN, preferred_element_type=jnp.float32
        )

    for o in range(1, CYCLE):
        qg_copy(o).wait_recv()
        q_total = q_total + qg_recv[o].astype(jnp.float32)
    g = jnp.transpose(q_total)
    raw = qraw[...]
    q_len = jnp.sqrt(jnp.sum(raw * raw, axis=1, keepdims=True) + EPSILON)
    v = raw / q_len
    raw_g = (g - v * jnp.sum(v * g, axis=1, keepdims=True)) / q_len
    term = term + lax.dot_general(
        raw_g.astype(jnp.bfloat16), qh_ref[...].reshape(q_rows, width), TN,
        preferred_element_type=jnp.float32,
    )
    whole = jnp.transpose(term)
    chunk = grad_ref.shape[0]
    for k in range(n):
        piece = whole[k * chunk : (k + 1) * chunk]
        part_own[k] = piece
        part[k] = piece.astype(link_dtype)

    def part_copy(k):
        return remote(part.at[peer(k)], part_recv.at[k], part_ss.at[k], part_rs.at[k], peer(k))

    @pl.loop(1, n)
    def _(k):
        part_copy(k).start()

    grad_ref[...] = part_own[me]

    @pl.loop(1, n)
    def _(k):
        part_copy(k).wait_recv()
        grad_ref[...] += part_recv[k].astype(jnp.float32)

    for o in range(1, CYCLE):
        q_copy(o).wait_send()
        s_copy(o).wait_send()
        g_copy(o).wait_send()
        qg_copy(o).wait_send()

    @pl.loop(1, n)
    def _(k):
        teach_send(k).wait_send()
        part_copy(k).wait_send()


def per_device(
    n, query_hidden, passage_hidden, projection, teacher_rows, teacher_pos, neg_count, pass_len
):
    queries, q_tokens, width = query_hidden.shape
    passages, p_tokens, _ = passage_hidden.shape
    dim = projection.shape[1]
    q_rows = queries * q_tokens
    padded = -(-p_tokens // 16) * 16
    p_rows = passages * padded
    chunk = width // n
    link_dtype = jnp.bfloat16
    f32, bf16 = jnp.float32, jnp.bfloat16
    vmem = pl.BlockSpec(memory_space=pltpu.VMEM)
    smem = pl.BlockSpec(memory_space=pltpu.SMEM)
    dma = pltpu.SemaphoreType.DMA
    loss, grad_w = pl.pallas_call(
        functools.partial(kernel, n, link_dtype),
        out_shape=(
            jax.ShapeDtypeStruct((1, queries), f32),
            jax.ShapeDtypeStruct((chunk, dim), f32),
        ),
        in_specs=[vmem] * 6 + [smem],
        out_specs=(vmem, vmem),
        scratch_shapes=[
            pltpu.VMEM((queries, 128), f32),
            pltpu.VMEM((n, queries, 128), f32),
            pltpu.VMEM((q_rows, dim), f32),
            pltpu.VMEM((CYCLE, q_rows, dim), bf16),
            pltpu.VMEM((p_rows, dim), f32),
            pltpu.VMEM((p_rows, dim), f32),
            pltpu.VMEM((p_rows, dim), bf16),
            pltpu.VMEM((CYCLE, p_rows, q_rows), f32),
            pltpu.VMEM((CYCLE, passages, q_rows), f32),
            pltpu.VMEM((p_rows, q_rows), bf16),
            pltpu.VMEM((p_rows, dim), f32),
            pltpu.VMEM((CYCLE, passages, 128), f32),
            pltpu.VMEM((CYCLE, passages, 128), f32),
            pltpu.VMEM((CYCLE, passages, 128), f32),
            pltpu.VMEM((CYCLE, passages, 128), f32),
            pltpu.VMEM((CYCLE, dim, q_rows), link_dtype),
            pltpu.VMEM((CYCLE, dim, q_rows), link_dtype),
            pltpu.VMEM((n, chunk, dim), link_dtype),
            pltpu.VMEM((n, chunk, dim), f32),
            pltpu.VMEM((n, chunk, dim), link_dtype),
            dma((n,)), dma((n,)),
            dma((CYCLE,)), dma((CYCLE,)),
            dma((CYCLE,)), dma((CYCLE,)),
            dma((CYCLE,)), dma((CYCLE,)),
            dma((CYCLE,)), dma((CYCLE,)),
            dma((n,)), dma((n,)),
        ],
        compiler_params=pltpu.CompilerParams(
            collective_id=0, has_side_effects=True, vmem_limit_bytes=50 * 1024 * 1024
        ),
    )(
        query_hidden,
        passage_hidden,
        projection,
        teacher_rows,
        teacher_pos.reshape(1, queries),
        neg_count.reshape(1, queries),
        pass_len.reshape(1, passages),
    )
    return (loss.reshape(queries), grad_w)


def solution(mesh):
    return jax.shard_map(
        functools.partial(per_device, mesh.shape["blk"]),
        mesh=mesh,
        in_specs=(
            P(("groups", "blk"), None, None),
            P(("groups", "blk"), None, None),
            P(),
            P(("groups", "blk"), None),
            P(("groups", "blk")),
            P(("groups", "blk")),
            P(("groups", "blk")),
        ),
        out_specs=(P(("groups", "blk")), P(("groups", "blk"), None)),
        check_vma=False,
    )
```

```python
import functools
import math

import jax
import jax.numpy as jnp
from jax import lax
from jax.experimental import pallas as pl
from jax.experimental.pallas import tpu as pltpu
from jax.sharding import PartitionSpec as P

CYCLE = 4
HEAT = 0.05
EPSILON = 1e-06
EXP2_SCALE = math.log2(math.e) / HEAT
NT = (((1,), (1,)), ((), ()))
TN = (((0,), (0,)), ((), ()))


def dot32(a, b, dims):
    return lax.dot_general(
        a, b, dims, precision=lax.Precision.HIGHEST, preferred_element_type=jnp.float32
    )


def kernel(
    n, link_dtype,
    qh_ref, ph_ref, proj_ref, rows_ref, pos_ref, cnt_ref, len_ref,
    loss_ref, grad_ref,
    teach_own, teach_all, qraw, q_all, pv, plen, pu, put, exps, den, w_buf, pgrad,
    s_send, s_recv, g_send, g_recv, qg_send, qg_recv, part, part_own, part_recv,
    teach_ss, teach_rs, q_ss, q_rs, s_ss, s_rs, g_ss, g_rs, qg_ss, qg_rs, part_ss, part_rs,
):
    me = lax.axis_index("blk")
    queries, q_tokens, width = qh_ref.shape
    p_tokens, passages, _ = ph_ref.shape
    dim = proj_ref.shape[1]
    q_rows = queries * q_tokens
    p_rows = p_tokens * passages
    step = next(t for t in (20, 12, 4, 2) if p_tokens % t == 0)
    block = step * passages

    def peer(shift):
        return lax.rem(me + shift + n, n)

    def remote(src, dst, ss, rs, target):
        return pltpu.make_async_remote_copy(
            src_ref=src, dst_ref=dst, send_sem=ss, recv_sem=rs,
            device_id={"blk": target}, device_id_type=pl.DeviceIdType.MESH,
        )

    barrier = pltpu.get_barrier_semaphore()

    @pl.loop(1, n)
    def _(k):
        pl.semaphore_signal(
            barrier, inc=1, device_id={"blk": peer(k)}, device_id_type=pl.DeviceIdType.MESH
        )

    projection = proj_ref[...]
    q_hidden = qh_ref[...].reshape(q_rows, width)
    raw = jnp.dot(q_hidden, projection, preferred_element_type=jnp.float32)
    qraw[...] = raw
    q_len = jnp.sqrt(jnp.sum(raw * raw, axis=1, keepdims=True) + EPSILON)
    q_all[0] = (raw / q_len).astype(jnp.bfloat16)
    teach_own[...] = jnp.zeros(teach_own.shape, jnp.float32)
    teach_own[:, : rows_ref.shape[1]] = rows_ref[...]
    teach_all[me] = teach_own[...]
    pl.semaphore_wait(barrier, n - 1)

    def q_copy(o):
        return remote(q_all.at[0], q_all.at[o], q_ss.at[o], q_rs.at[o], peer(o))

    for o in range(1, CYCLE):
        q_copy(o).start()

    def teach_send(k):
        return remote(teach_own, teach_all.at[me], teach_ss.at[k], teach_rs.at[k], peer(k))

    def teach_recv(k):
        return remote(teach_own, teach_all.at[peer(-k)], teach_ss.at[k], teach_rs.at[k], peer(k))

    @pl.loop(1, n)
    def _(k):
        teach_send(k).start()

    p_hidden = ph_ref[...].reshape(p_rows, width)
    raw_p = jnp.dot(p_hidden, projection, preferred_element_type=jnp.float32)
    length = jnp.sqrt(jnp.sum(raw_p * raw_p, axis=1, keepdims=True) + EPSILON)
    units_p = raw_p / length
    pv[...] = units_p
    plen[...] = jnp.broadcast_to(length, raw_p.shape)
    pu[...] = units_p.astype(jnp.bfloat16)
    put[...] = jnp.transpose(units_p).astype(jnp.bfloat16)

    low = lax.broadcasted_iota(jnp.int32, (queries, q_rows), 0) * q_tokens
    lane = lax.broadcasted_iota(jnp.int32, (queries, q_rows), 1)
    spread = jnp.where((lane >= low) & (lane < low + q_tokens), 1.0, 0.0)
    passage = lax.broadcasted_iota(jnp.int32, (passages, q_rows), 0)
    limit = jnp.zeros((passages, q_rows), jnp.int32)
    for p in range(passages):
        limit = jnp.where(passage == p, len_ref[0, p], limit)
    token = lax.broadcasted_iota(jnp.int32, (step, passages, q_rows), 0)

    s_send[...] = jnp.zeros(s_send.shape, jnp.float32)
    g_send[...] = jnp.zeros(g_send.shape, jnp.float32)

    def s_copy(o):
        return remote(s_send.at[o], s_recv.at[o], s_ss.at[o], s_rs.at[o], peer(-o))

    def g_copy(o):
        return remote(g_send.at[o], g_recv.at[o], g_ss.at[o], g_rs.at[o], peer(o))

    def qg_copy(o):
        return remote(qg_send.at[o], qg_recv.at[o], qg_ss.at[o], qg_rs.at[o], peer(-o))

    def score(o):
        units = q_all[o]

        def body(k, total):
            at = pl.ds(pl.multiple_of(k * block, block), block)
            sims = lax.dot_general(pu[at], units, NT, preferred_element_type=jnp.float32)
            sims = sims.reshape(step, passages, q_rows)
            e = jnp.where(token < (limit - k * step)[None], jnp.exp2(sims * EXP2_SCALE), 0.0)
            exps[o, pl.ds(k * step, step)] = e
            return total + jnp.sum(e, axis=0)

        den[o] = lax.fori_loop(
            0, p_tokens // step, body, jnp.zeros((passages, q_rows), jnp.float32)
        )
        peaks = HEAT * jnp.log(den[o])
        return dot32(peaks, spread, NT)

    own_scores = score(0)
    for o in range(1, CYCLE):
        q_copy(o).wait_recv()
        s_send[o, :, :queries] = score(o)
        s_copy(o).start()

    @pl.loop(1, n)
    def _(k):
        teach_recv(k).wait_recv()

    stored = teach_all[...].reshape(n * queries, teach_all.shape[2])
    cand = CYCLE * passages
    rows = lax.broadcasted_iota(jnp.int32, (n * queries, queries), 0)
    pick = jnp.where(rows == pos_ref[...], 1.0, 0.0)
    teacher = dot32(jnp.transpose(stored)[:cand], pick, (((1,), (0,)), ((), ())))
    valid = lax.broadcasted_iota(jnp.int32, (cand, queries), 0) < cnt_ref[...]
    teacher_exp = jnp.where(valid, jnp.exp(teacher), 0.0)
    teacher_total = jnp.sum(teacher_exp, axis=0, keepdims=True)
    teacher_prob = teacher_exp / teacher_total
    teacher_log = teacher - jnp.log(teacher_total)

    student_parts = [own_scores]
    for o in range(1, CYCLE):
        s_copy(o).wait_recv()
        student_parts.append(s_recv[o, :, :queries])
    student = jnp.concatenate(student_parts, axis=0)
    student_exp = jnp.where(valid, jnp.exp(student), 0.0)
    student_total = jnp.sum(student_exp, axis=0, keepdims=True)
    score_grad = student_exp / student_total - teacher_prob
    for o in range(1, CYCLE):
        g_send[o, :, :queries] = score_grad[o * passages : (o + 1) * passages]
        g_copy(o).start()
    gap = teacher_log - (student - jnp.log(student_total))
    loss_ref[...] = jnp.sum(jnp.where(valid, teacher_prob * gap, 0.0), axis=0, keepdims=True)

    def backward(o, grads):
        units = q_all[o]
        scale = dot32(grads, spread, (((1,), (0,)), ((), ()))) / den[o]

        @pl.loop(0, p_tokens // step)
        def _(k):
            at = pl.ds(pl.multiple_of(k * block, block), block)
            w = exps[o, pl.ds(k * step, step)] * scale[None]
            w = w.reshape(block, q_rows).astype(jnp.bfloat16)
            w_buf[at] = w
            part_grad = jnp.dot(w, units, preferred_element_type=jnp.float32)
            if o == 0:
                pgrad[at] = part_grad
            else:
                pgrad[at] += part_grad

        return jnp.dot(put[...], w_buf[...], preferred_element_type=jnp.float32)

    q_total = backward(0, score_grad[:passages])
    for o in range(1, CYCLE):
        g_copy(o).wait_recv()
        qg_send[o] = backward(o, g_recv[o, :, :queries]).astype(link_dtype)
        qg_copy(o).start()

    v_p = pv[...]
    g_p = pgrad[...]
    raw_g = (g_p - v_p * jnp.sum(v_p * g_p, axis=1, keepdims=True)) / plen[...]
    term = lax.dot_general(
        raw_g.astype(jnp.bfloat16), ph_ref[...].reshape(p_rows, width), TN,
        preferred_element_type=jnp.float32,
    )

    for o in range(1, CYCLE):
        qg_copy(o).wait_recv()
        q_total = q_total + qg_recv[o].astype(jnp.float32)
    g = jnp.transpose(q_total)
    raw = qraw[...]
    q_len = jnp.sqrt(jnp.sum(raw * raw, axis=1, keepdims=True) + EPSILON)
    v = raw / q_len
    raw_g = (g - v * jnp.sum(v * g, axis=1, keepdims=True)) / q_len
    term = term + lax.dot_general(
        raw_g.astype(jnp.bfloat16), qh_ref[...].reshape(q_rows, width), TN,
        preferred_element_type=jnp.float32,
    )
    whole = jnp.transpose(term)
    chunk = grad_ref.shape[0]
    for k in range(n):
        piece = whole[k * chunk : (k + 1) * chunk]
        part_own[k] = piece
        part[k] = piece.astype(link_dtype)

    def part_copy(k):
        return remote(part.at[peer(k)], part_recv.at[k], part_ss.at[k], part_rs.at[k], peer(k))

    @pl.loop(1, n)
    def _(k):
        part_copy(k).start()

    grad_ref[...] = part_own[me]

    @pl.loop(1, n)
    def _(k):
        part_copy(k).wait_recv()
        grad_ref[...] += part_recv[k].astype(jnp.float32)

    for o in range(1, CYCLE):
        q_copy(o).wait_send()
        s_copy(o).wait_send()
        g_copy(o).wait_send()
        qg_copy(o).wait_send()

    @pl.loop(1, n)
    def _(k):
        teach_send(k).wait_send()
        part_copy(k).wait_send()


def per_device(
    n, query_hidden, passage_hidden, projection, teacher_rows, teacher_pos, neg_count, pass_len
):
    queries, q_tokens, width = query_hidden.shape
    passages, p_tokens, _ = passage_hidden.shape
    dim = projection.shape[1]
    q_rows = queries * q_tokens
    p_rows = passages * p_tokens
    chunk = width // n
    link_dtype = jnp.bfloat16
    f32, bf16 = jnp.float32, jnp.bfloat16
    vmem = pl.BlockSpec(memory_space=pltpu.VMEM)
    smem = pl.BlockSpec(memory_space=pltpu.SMEM)
    dma = pltpu.SemaphoreType.DMA
    loss, grad_w = pl.pallas_call(
        functools.partial(kernel, n, link_dtype),
        out_shape=(
            jax.ShapeDtypeStruct((1, queries), f32),
            jax.ShapeDtypeStruct((chunk, dim), f32),
        ),
        in_specs=[vmem] * 6 + [smem],
        out_specs=(vmem, vmem),
        scratch_shapes=[
            pltpu.VMEM((queries, 128), f32),
            pltpu.VMEM((n, queries, 128), f32),
            pltpu.VMEM((q_rows, dim), f32),
            pltpu.VMEM((CYCLE, q_rows, dim), bf16),
            pltpu.VMEM((p_rows, dim), f32),
            pltpu.VMEM((p_rows, dim), f32),
            pltpu.VMEM((p_rows, dim), bf16),
            pltpu.VMEM((dim, p_rows), bf16),
            pltpu.VMEM((CYCLE, p_tokens, passages, q_rows), f32),
            pltpu.VMEM((CYCLE, passages, q_rows), f32),
            pltpu.VMEM((p_rows, q_rows), bf16),
            pltpu.VMEM((p_rows, dim), f32),
            pltpu.VMEM((CYCLE, passages, 128), f32),
            pltpu.VMEM((CYCLE, passages, 128), f32),
            pltpu.VMEM((CYCLE, passages, 128), f32),
            pltpu.VMEM((CYCLE, passages, 128), f32),
            pltpu.VMEM((CYCLE, dim, q_rows), link_dtype),
            pltpu.VMEM((CYCLE, dim, q_rows), link_dtype),
            pltpu.VMEM((n, chunk, dim), link_dtype),
            pltpu.VMEM((n, chunk, dim), f32),
            pltpu.VMEM((n, chunk, dim), link_dtype),
            dma((n,)), dma((n,)),
            dma((CYCLE,)), dma((CYCLE,)),
            dma((CYCLE,)), dma((CYCLE,)),
            dma((CYCLE,)), dma((CYCLE,)),
            dma((CYCLE,)), dma((CYCLE,)),
            dma((n,)), dma((n,)),
        ],
        compiler_params=pltpu.CompilerParams(
            collective_id=0, has_side_effects=True, vmem_limit_bytes=50 * 1024 * 1024
        ),
    )(
        query_hidden,
        jnp.transpose(passage_hidden, (1, 0, 2)),
        projection,
        teacher_rows,
        teacher_pos.reshape(1, queries),
        neg_count.reshape(1, queries),
        pass_len.reshape(1, passages),
    )
    return (loss.reshape(queries), grad_w)


def solution(mesh):
    return jax.shard_map(
        functools.partial(per_device, mesh.shape["blk"]),
        mesh=mesh,
        in_specs=(
            P(("groups", "blk"), None, None),
            P(("groups", "blk"), None, None),
            P(),
            P(("groups", "blk"), None),
            P(("groups", "blk")),
            P(("groups", "blk")),
            P(("groups", "blk")),
        ),
        out_specs=(P(("groups", "blk")), P(("groups", "blk"), None)),
        check_vma=False,
    )
```

```python
import functools

import jax
import jax.numpy as jnp
from jax import lax
from jax.experimental import pallas as pl
from jax.experimental.pallas import tpu as pltpu
from jax.sharding import PartitionSpec as P

CYCLE = 4
HEAT = 0.05
EPSILON = 1e-06
NT = (((1,), (1,)), ((), ()))
TN = (((0,), (0,)), ((), ()))


def dot32(a, b, dims):
    return lax.dot_general(
        a, b, dims, precision=lax.Precision.HIGHEST, preferred_element_type=jnp.float32
    )


def kernel(
    n, link_dtype,
    qh_ref, ph_ref, proj_ref, rows_ref, pos_ref, cnt_ref, len_ref,
    loss_ref, grad_ref,
    teach_own, teach_all, qraw, q_all, pv, plen, pu, put, exps, den, w_buf, pgrad,
    s_send, s_recv, g_send, g_recv, qg_send, qg_recv, part, part_own, part_recv,
    teach_ss, teach_rs, q_ss, q_rs, s_ss, s_rs, g_ss, g_rs, qg_ss, qg_rs, part_ss, part_rs,
):
    me = lax.axis_index("blk")
    queries, q_tokens, width = qh_ref.shape
    passages = len_ref.shape[1]
    p_tokens = ph_ref.shape[0] // passages
    dim = proj_ref.shape[1]
    q_rows = queries * q_tokens
    p_rows = ph_ref.shape[0]

    def peer(shift):
        return lax.rem(me + shift + n, n)

    def remote(src, dst, ss, rs, target):
        return pltpu.make_async_remote_copy(
            src_ref=src, dst_ref=dst, send_sem=ss, recv_sem=rs,
            device_id={"blk": target}, device_id_type=pl.DeviceIdType.MESH,
        )

    barrier = pltpu.get_barrier_semaphore()

    @pl.loop(1, n)
    def _(k):
        pl.semaphore_signal(
            barrier, inc=1, device_id={"blk": peer(k)}, device_id_type=pl.DeviceIdType.MESH
        )

    projection = proj_ref[...]
    q_hidden = qh_ref[...].reshape(q_rows, width)
    raw = jnp.dot(q_hidden, projection, preferred_element_type=jnp.float32)
    qraw[...] = raw
    q_len = jnp.sqrt(jnp.sum(raw * raw, axis=1, keepdims=True) + EPSILON)
    q_all[0] = (raw / q_len).astype(jnp.bfloat16)
    teach_own[...] = jnp.zeros(teach_own.shape, jnp.float32)
    teach_own[:, : rows_ref.shape[1]] = rows_ref[...]
    teach_all[me] = teach_own[...]
    raw_p = jnp.dot(ph_ref[...], projection, preferred_element_type=jnp.float32)
    length = jnp.sqrt(jnp.sum(raw_p * raw_p, axis=1, keepdims=True) + EPSILON)
    units_p = raw_p / length
    pv[...] = units_p
    plen[...] = jnp.broadcast_to(length, raw_p.shape)
    pu[...] = units_p.astype(jnp.bfloat16)
    put[...] = jnp.transpose(units_p).astype(jnp.bfloat16)

    pl.semaphore_wait(barrier, n - 1)

    def q_copy(o):
        return remote(q_all.at[0], q_all.at[o], q_ss.at[o], q_rs.at[o], peer(o))

    for o in range(1, CYCLE):
        q_copy(o).start()

    def teach_send(k):
        return remote(teach_own, teach_all.at[me], teach_ss.at[k], teach_rs.at[k], peer(k))

    def teach_recv(k):
        return remote(teach_own, teach_all.at[peer(-k)], teach_ss.at[k], teach_rs.at[k], peer(k))

    @pl.loop(1, n)
    def _(k):
        teach_send(k).start()

    low = lax.broadcasted_iota(jnp.int32, (queries, q_rows), 0) * q_tokens
    lane = lax.broadcasted_iota(jnp.int32, (queries, q_rows), 1)
    spread = jnp.where((lane >= low) & (lane < low + q_tokens), 1.0, 0.0)
    passage = lax.broadcasted_iota(jnp.int32, (passages, q_rows), 0)
    limit = jnp.zeros((passages, q_rows), jnp.int32)
    for p in range(passages):
        limit = jnp.where(passage == p, len_ref[0, p], limit)

    s_send[...] = jnp.zeros(s_send.shape, jnp.float32)
    g_send[...] = jnp.zeros(g_send.shape, jnp.float32)

    def s_copy(o):
        return remote(s_send.at[o], s_recv.at[o], s_ss.at[o], s_rs.at[o], peer(-o))

    def g_copy(o):
        return remote(g_send.at[o], g_recv.at[o], g_ss.at[o], g_rs.at[o], peer(o))

    def qg_copy(o):
        return remote(qg_send.at[o], qg_recv.at[o], qg_ss.at[o], qg_rs.at[o], peer(-o))

    def score(o):
        units = q_all[o]

        sims = lax.dot_general(pu[...], units, NT, preferred_element_type=jnp.float32)
        total = jnp.zeros((passages, q_rows), jnp.float32)
        for t in range(p_tokens):
            e = jnp.exp(sims[t * passages : (t + 1) * passages] * (1.0 / HEAT))
            e = jnp.where(limit > t, e, 0.0)
            exps[o, t] = e
            total = total + e
        den[o] = total
        peaks = HEAT * jnp.log(den[o])
        return dot32(peaks, spread, NT)

    own_scores = score(0)
    for o in range(1, CYCLE):
        q_copy(o).wait_recv()
        s_send[o, :, :queries] = score(o)
        s_copy(o).start()

    @pl.loop(1, n)
    def _(k):
        teach_recv(k).wait_recv()

    stored = teach_all[...].reshape(n * queries, teach_all.shape[2])
    cand = CYCLE * passages
    rows = lax.broadcasted_iota(jnp.int32, (n * queries, queries), 0)
    pick = jnp.where(rows == pos_ref[...], 1.0, 0.0)
    teacher = dot32(jnp.transpose(stored)[:cand], pick, (((1,), (0,)), ((), ())))
    valid = lax.broadcasted_iota(jnp.int32, (cand, queries), 0) < cnt_ref[...]
    teacher_exp = jnp.where(valid, jnp.exp(teacher), 0.0)
    teacher_total = jnp.sum(teacher_exp, axis=0, keepdims=True)
    teacher_prob = teacher_exp / teacher_total
    teacher_log = teacher - jnp.log(teacher_total)

    student_parts = [own_scores]
    for o in range(1, CYCLE):
        s_copy(o).wait_recv()
        student_parts.append(s_recv[o, :, :queries])
    student = jnp.concatenate(student_parts, axis=0)
    student_exp = jnp.where(valid, jnp.exp(student), 0.0)
    student_total = jnp.sum(student_exp, axis=0, keepdims=True)
    score_grad = student_exp / student_total - teacher_prob
    for o in range(1, CYCLE):
        g_send[o, :, :queries] = score_grad[o * passages : (o + 1) * passages]
        g_copy(o).start()
    gap = teacher_log - (student - jnp.log(student_total))
    loss_ref[...] = jnp.sum(jnp.where(valid, teacher_prob * gap, 0.0), axis=0, keepdims=True)

    def backward(o, grads):
        units = q_all[o]
        scale = dot32(grads, spread, (((1,), (0,)), ((), ()))) / den[o]

        w = (exps[o] * scale[None]).reshape(p_rows, q_rows).astype(jnp.bfloat16)
        w_buf[...] = w
        q_grad = jnp.dot(put[...], w_buf[...], preferred_element_type=jnp.float32)
        if o > 0:
            qg_send[o] = q_grad.astype(link_dtype)
            qg_copy(o).start()
        part_grad = jnp.dot(w_buf[...], units, preferred_element_type=jnp.float32)
        if o == 0:
            pgrad[...] = part_grad
        else:
            pgrad[...] += part_grad
        return q_grad

    q_total = backward(0, score_grad[:passages])
    for o in range(1, CYCLE):
        g_copy(o).wait_recv()
        backward(o, g_recv[o, :, :queries])

    v_p = pv[...]
    g_p = pgrad[...]
    raw_g = (g_p - v_p * jnp.sum(v_p * g_p, axis=1, keepdims=True)) / plen[...]
    term = lax.dot_general(
        raw_g.astype(jnp.bfloat16), ph_ref[...], TN,
        preferred_element_type=jnp.float32,
    )

    for o in range(1, CYCLE):
        qg_copy(o).wait_recv()
        q_total = q_total + qg_recv[o].astype(jnp.float32)
    g = jnp.transpose(q_total)
    raw = qraw[...]
    q_len = jnp.sqrt(jnp.sum(raw * raw, axis=1, keepdims=True) + EPSILON)
    v = raw / q_len
    raw_g = (g - v * jnp.sum(v * g, axis=1, keepdims=True)) / q_len
    term = term + lax.dot_general(
        raw_g.astype(jnp.bfloat16), qh_ref[...].reshape(q_rows, width), TN,
        preferred_element_type=jnp.float32,
    )
    whole = jnp.transpose(term)
    chunk = grad_ref.shape[0]
    for k in range(n):
        piece = whole[k * chunk : (k + 1) * chunk]
        part_own[k] = piece
        part[k] = piece.astype(link_dtype)

    def part_copy(k):
        return remote(part.at[peer(k)], part_recv.at[k], part_ss.at[k], part_rs.at[k], peer(k))

    @pl.loop(1, n)
    def _(k):
        part_copy(k).start()

    grad_ref[...] = part_own[me]

    @pl.loop(1, n)
    def _(k):
        part_copy(k).wait_recv()
        grad_ref[...] += part_recv[k].astype(jnp.float32)

    for o in range(1, CYCLE):
        q_copy(o).wait_send()
        s_copy(o).wait_send()
        g_copy(o).wait_send()
        qg_copy(o).wait_send()

    @pl.loop(1, n)
    def _(k):
        teach_send(k).wait_send()
        part_copy(k).wait_send()


def per_device(
    n, query_hidden, passage_hidden, projection, teacher_rows, teacher_pos, neg_count, pass_len
):
    queries, q_tokens, width = query_hidden.shape
    passages, p_tokens, _ = passage_hidden.shape
    dim = projection.shape[1]
    q_rows = queries * q_tokens
    p_rows = passages * p_tokens
    chunk = width // n
    link_dtype = jnp.bfloat16
    f32, bf16 = jnp.float32, jnp.bfloat16
    vmem = pl.BlockSpec(memory_space=pltpu.VMEM)
    smem = pl.BlockSpec(memory_space=pltpu.SMEM)
    dma = pltpu.SemaphoreType.DMA
    loss, grad_w = pl.pallas_call(
        functools.partial(kernel, n, link_dtype),
        out_shape=(
            jax.ShapeDtypeStruct((1, queries), f32),
            jax.ShapeDtypeStruct((chunk, dim), f32),
        ),
        in_specs=[vmem] * 6 + [smem],
        out_specs=(vmem, vmem),
        scratch_shapes=[
            pltpu.VMEM((queries, 128), f32),
            pltpu.VMEM((n, queries, 128), f32),
            pltpu.VMEM((q_rows, dim), f32),
            pltpu.VMEM((CYCLE, q_rows, dim), bf16),
            pltpu.VMEM((p_rows, dim), f32),
            pltpu.VMEM((p_rows, dim), f32),
            pltpu.VMEM((p_rows, dim), bf16),
            pltpu.VMEM((dim, p_rows), bf16),
            pltpu.VMEM((CYCLE, p_tokens, passages, q_rows), f32),
            pltpu.VMEM((CYCLE, passages, q_rows), f32),
            pltpu.VMEM((p_rows, q_rows), bf16),
            pltpu.VMEM((p_rows, dim), f32),
            pltpu.VMEM((CYCLE, passages, 128), f32),
            pltpu.VMEM((CYCLE, passages, 128), f32),
            pltpu.VMEM((CYCLE, passages, 128), f32),
            pltpu.VMEM((CYCLE, passages, 128), f32),
            pltpu.VMEM((CYCLE, dim, q_rows), link_dtype),
            pltpu.VMEM((CYCLE, dim, q_rows), link_dtype),
            pltpu.VMEM((n, chunk, dim), link_dtype),
            pltpu.VMEM((n, chunk, dim), f32),
            pltpu.VMEM((n, chunk, dim), link_dtype),
            dma((n,)), dma((n,)),
            dma((CYCLE,)), dma((CYCLE,)),
            dma((CYCLE,)), dma((CYCLE,)),
            dma((CYCLE,)), dma((CYCLE,)),
            dma((CYCLE,)), dma((CYCLE,)),
            dma((n,)), dma((n,)),
        ],
        compiler_params=pltpu.CompilerParams(
            collective_id=0, has_side_effects=True, vmem_limit_bytes=50 * 1024 * 1024
        ),
    )(
        query_hidden,
        jnp.transpose(passage_hidden, (1, 0, 2)).reshape(p_rows, width),
        projection,
        teacher_rows,
        teacher_pos.reshape(1, queries),
        neg_count.reshape(1, queries),
        pass_len.reshape(1, passages),
    )
    return (loss.reshape(queries), grad_w)


def solution(mesh):
    return jax.shard_map(
        functools.partial(per_device, mesh.shape["blk"]),
        mesh=mesh,
        in_specs=(
            P(("groups", "blk"), None, None),
            P(("groups", "blk"), None, None),
            P(),
            P(("groups", "blk"), None),
            P(("groups", "blk")),
            P(("groups", "blk")),
            P(("groups", "blk")),
        ),
        out_specs=(P(("groups", "blk")), P(("groups", "blk"), None)),
        check_vma=False,
    )
```

```python
import functools

import jax
import jax.numpy as jnp
from jax import lax
from jax.experimental import pallas as pl
from jax.experimental.pallas import tpu as pltpu
from jax.sharding import PartitionSpec as P

CYCLE = 4
HEAT = 0.05
EPSILON = 1e-06
NT = (((1,), (1,)), ((), ()))
TN = (((0,), (0,)), ((), ()))


def dot32(a, b, dims):
    return lax.dot_general(
        a, b, dims, precision=lax.Precision.HIGHEST, preferred_element_type=jnp.float32
    )


def kernel(
    n, link_dtype,
    qh_ref, ph_ref, proj_ref, rows_ref, pos_ref, cnt_ref, len_ref,
    loss_ref, grad_ref,
    teach_own, teach_all, qraw, q_all, pv, plen, pu, exps, den, w_buf, pgrad,
    s_send, s_recv, g_send, g_recv, qg_send, qg_recv, part, part_own, part_recv,
    teach_ss, teach_rs, q_ss, q_rs, s_ss, s_rs, g_ss, g_rs, qg_ss, qg_rs, part_ss, part_rs,
):
    me = lax.axis_index("blk")
    queries, q_tokens, width = qh_ref.shape
    passages, p_tokens, _ = ph_ref.shape
    dim = proj_ref.shape[1]
    q_rows = queries * q_tokens
    padded = pu.shape[0] // passages

    def peer(shift):
        return lax.rem(me + shift + n, n)

    def remote(src, dst, ss, rs, target):
        return pltpu.make_async_remote_copy(
            src_ref=src, dst_ref=dst, send_sem=ss, recv_sem=rs,
            device_id={"blk": target}, device_id_type=pl.DeviceIdType.MESH,
        )

    barrier = pltpu.get_barrier_semaphore()

    @pl.loop(1, n)
    def _(k):
        pl.semaphore_signal(
            barrier, inc=1, device_id={"blk": peer(k)}, device_id_type=pl.DeviceIdType.MESH
        )

    projection = proj_ref[...]
    q_hidden = qh_ref[...].reshape(q_rows, width)
    raw = jnp.dot(q_hidden, projection, preferred_element_type=jnp.float32)
    qraw[...] = raw
    q_len = jnp.sqrt(jnp.sum(raw * raw, axis=1, keepdims=True) + EPSILON)
    q_all[0] = (raw / q_len).astype(jnp.bfloat16)
    teach_own[...] = jnp.zeros(teach_own.shape, jnp.float32)
    teach_own[:, : rows_ref.shape[1]] = rows_ref[...]
    teach_all[me] = teach_own[...]
    pl.semaphore_wait(barrier, n - 1)

    def q_copy(o):
        return remote(q_all.at[0], q_all.at[o], q_ss.at[o], q_rs.at[o], peer(o))

    for o in range(1, CYCLE):
        q_copy(o).start()

    def teach_send(k):
        return remote(teach_own, teach_all.at[me], teach_ss.at[k], teach_rs.at[k], peer(k))

    def teach_recv(k):
        return remote(teach_own, teach_all.at[peer(-k)], teach_ss.at[k], teach_rs.at[k], peer(k))

    @pl.loop(1, n)
    def _(k):
        teach_send(k).start()

    pv[...] = jnp.zeros(pv.shape, jnp.float32)
    plen[...] = jnp.ones(plen.shape, jnp.float32)

    for p in range(passages):
        at = p * padded
        raw_p = jnp.dot(ph_ref[p], projection, preferred_element_type=jnp.float32)
        length = jnp.sqrt(jnp.sum(raw_p * raw_p, axis=1, keepdims=True) + EPSILON)
        pv[at : at + p_tokens] = raw_p / length
        plen[at : at + p_tokens] = jnp.broadcast_to(length, raw_p.shape)
    pu[...] = pv[...].astype(jnp.bfloat16)
    pgrad[...] = jnp.zeros(pgrad.shape, jnp.float32)

    low = lax.broadcasted_iota(jnp.int32, (queries, q_rows), 0) * q_tokens
    lane = lax.broadcasted_iota(jnp.int32, (queries, q_rows), 1)
    spread = jnp.where((lane >= low) & (lane < low + q_tokens), 1.0, 0.0)
    token = lax.broadcasted_iota(jnp.int32, (padded, q_rows), 0)

    s_send[...] = jnp.zeros(s_send.shape, jnp.float32)
    g_send[...] = jnp.zeros(g_send.shape, jnp.float32)

    def s_copy(o):
        return remote(s_send.at[o], s_recv.at[o], s_ss.at[o], s_rs.at[o], peer(-o))

    def g_copy(o):
        return remote(g_send.at[o], g_recv.at[o], g_ss.at[o], g_rs.at[o], peer(o))

    def qg_copy(o):
        return remote(qg_send.at[o], qg_recv.at[o], qg_ss.at[o], qg_rs.at[o], peer(-o))

    def score(o):
        units = q_all[o]

        @pl.loop(0, passages, unroll=8)
        def _(p):
            at = pl.ds(pl.multiple_of(p * padded, padded), padded)
            sims = lax.dot_general(pu[at], units, NT, preferred_element_type=jnp.float32)
            e = jnp.where(token < len_ref[0, p], jnp.exp(sims * (1.0 / HEAT)), 0.0)
            exps[o, at] = e
            den[o, pl.ds(p, 1)] = jnp.sum(e, axis=0, keepdims=True)

        peaks = HEAT * jnp.log(den[o])
        return dot32(peaks, spread, NT)

    own_scores = score(0)
    for o in range(1, CYCLE):
        q_copy(o).wait_recv()
        s_send[o, :, :queries] = score(o)
        s_copy(o).start()

    @pl.loop(1, n)
    def _(k):
        teach_recv(k).wait_recv()

    stored = teach_all[...].reshape(n * queries, teach_all.shape[2])
    cand = CYCLE * passages
    rows = lax.broadcasted_iota(jnp.int32, (n * queries, queries), 0)
    pick = jnp.where(rows == pos_ref[...], 1.0, 0.0)
    teacher = dot32(jnp.transpose(stored)[:cand], pick, (((1,), (0,)), ((), ())))
    valid = lax.broadcasted_iota(jnp.int32, (cand, queries), 0) < cnt_ref[...]
    teacher_exp = jnp.where(valid, jnp.exp(teacher), 0.0)
    teacher_total = jnp.sum(teacher_exp, axis=0, keepdims=True)
    teacher_prob = teacher_exp / teacher_total
    teacher_log = teacher - jnp.log(teacher_total)

    student_parts = [own_scores]
    for o in range(1, CYCLE):
        s_copy(o).wait_recv()
        student_parts.append(s_recv[o, :, :queries])
    student = jnp.concatenate(student_parts, axis=0)
    student_exp = jnp.where(valid, jnp.exp(student), 0.0)
    student_total = jnp.sum(student_exp, axis=0, keepdims=True)
    score_grad = student_exp / student_total - teacher_prob
    for o in range(1, CYCLE):
        g_send[o, :, :queries] = score_grad[o * passages : (o + 1) * passages]
        g_copy(o).start()
    gap = teacher_log - (student - jnp.log(student_total))
    loss_ref[...] = jnp.sum(jnp.where(valid, teacher_prob * gap, 0.0), axis=0, keepdims=True)

    def backward(o, grads):
        units = q_all[o]
        den[o] = dot32(grads, spread, (((1,), (0,)), ((), ()))) / den[o]

        @pl.loop(0, passages, unroll=8)
        def _(p):
            at = pl.ds(pl.multiple_of(p * padded, padded), padded)
            w = (exps[o, at] * den[o, pl.ds(p, 1)]).astype(jnp.bfloat16)
            w_buf[at] = w
            pgrad[at] += jnp.dot(w, units, preferred_element_type=jnp.float32)

        return lax.dot_general(pu[...], w_buf[...], TN, preferred_element_type=jnp.float32)

    q_total = backward(0, score_grad[:passages])
    for o in range(1, CYCLE):
        g_copy(o).wait_recv()
        qg_send[o] = backward(o, g_recv[o, :, :queries]).astype(link_dtype)
        qg_copy(o).start()

    term = jnp.zeros((dim, width), jnp.float32)
    for p in range(passages):
        at = p * padded
        v = pv[at : at + p_tokens]
        g = pgrad[at : at + p_tokens]
        raw_g = (g - v * jnp.sum(v * g, axis=1, keepdims=True)) / plen[at : at + p_tokens]
        term = term + lax.dot_general(
            raw_g.astype(jnp.bfloat16), ph_ref[p], TN, preferred_element_type=jnp.float32
        )

    for o in range(1, CYCLE):
        qg_copy(o).wait_recv()
        q_total = q_total + qg_recv[o].astype(jnp.float32)
    g = jnp.transpose(q_total)
    raw = qraw[...]
    q_len = jnp.sqrt(jnp.sum(raw * raw, axis=1, keepdims=True) + EPSILON)
    v = raw / q_len
    raw_g = (g - v * jnp.sum(v * g, axis=1, keepdims=True)) / q_len
    term = term + lax.dot_general(
        raw_g.astype(jnp.bfloat16), qh_ref[...].reshape(q_rows, width), TN,
        preferred_element_type=jnp.float32,
    )
    whole = jnp.transpose(term)
    chunk = grad_ref.shape[0]
    for k in range(n):
        piece = whole[k * chunk : (k + 1) * chunk]
        part_own[k] = piece
        part[k] = piece.astype(link_dtype)

    def part_copy(k):
        return remote(part.at[peer(k)], part_recv.at[k], part_ss.at[k], part_rs.at[k], peer(k))

    @pl.loop(1, n)
    def _(k):
        part_copy(k).start()

    grad_ref[...] = part_own[me]

    @pl.loop(1, n)
    def _(k):
        part_copy(k).wait_recv()
        grad_ref[...] += part_recv[k].astype(jnp.float32)

    for o in range(1, CYCLE):
        q_copy(o).wait_send()
        s_copy(o).wait_send()
        g_copy(o).wait_send()
        qg_copy(o).wait_send()

    @pl.loop(1, n)
    def _(k):
        teach_send(k).wait_send()
        part_copy(k).wait_send()


def per_device(
    n, query_hidden, passage_hidden, projection, teacher_rows, teacher_pos, neg_count, pass_len
):
    queries, q_tokens, width = query_hidden.shape
    passages, p_tokens, _ = passage_hidden.shape
    dim = projection.shape[1]
    q_rows = queries * q_tokens
    padded = -(-p_tokens // 16) * 16
    p_rows = passages * padded
    chunk = width // n
    link_dtype = jnp.bfloat16
    f32, bf16 = jnp.float32, jnp.bfloat16
    vmem = pl.BlockSpec(memory_space=pltpu.VMEM)
    smem = pl.BlockSpec(memory_space=pltpu.SMEM)
    dma = pltpu.SemaphoreType.DMA
    loss, grad_w = pl.pallas_call(
        functools.partial(kernel, n, link_dtype),
        out_shape=(
            jax.ShapeDtypeStruct((1, queries), f32),
            jax.ShapeDtypeStruct((chunk, dim), f32),
        ),
        in_specs=[vmem] * 6 + [smem],
        out_specs=(vmem, vmem),
        scratch_shapes=[
            pltpu.VMEM((queries, 128), f32),
            pltpu.VMEM((n, queries, 128), f32),
            pltpu.VMEM((q_rows, dim), f32),
            pltpu.VMEM((CYCLE, q_rows, dim), bf16),
            pltpu.VMEM((p_rows, dim), f32),
            pltpu.VMEM((p_rows, dim), f32),
            pltpu.VMEM((p_rows, dim), bf16),
            pltpu.VMEM((CYCLE, p_rows, q_rows), f32),
            pltpu.VMEM((CYCLE, passages, q_rows), f32),
            pltpu.VMEM((p_rows, q_rows), bf16),
            pltpu.VMEM((p_rows, dim), f32),
            pltpu.VMEM((CYCLE, passages, 128), f32),
            pltpu.VMEM((CYCLE, passages, 128), f32),
            pltpu.VMEM((CYCLE, passages, 128), f32),
            pltpu.VMEM((CYCLE, passages, 128), f32),
            pltpu.VMEM((CYCLE, dim, q_rows), link_dtype),
            pltpu.VMEM((CYCLE, dim, q_rows), link_dtype),
            pltpu.VMEM((n, chunk, dim), link_dtype),
            pltpu.VMEM((n, chunk, dim), f32),
            pltpu.VMEM((n, chunk, dim), link_dtype),
            dma((n,)), dma((n,)),
            dma((CYCLE,)), dma((CYCLE,)),
            dma((CYCLE,)), dma((CYCLE,)),
            dma((CYCLE,)), dma((CYCLE,)),
            dma((CYCLE,)), dma((CYCLE,)),
            dma((n,)), dma((n,)),
        ],
        compiler_params=pltpu.CompilerParams(
            collective_id=0, has_side_effects=True, vmem_limit_bytes=50 * 1024 * 1024
        ),
    )(
        query_hidden,
        passage_hidden,
        projection,
        teacher_rows,
        teacher_pos.reshape(1, queries),
        neg_count.reshape(1, queries),
        pass_len.reshape(1, passages),
    )
    return (loss.reshape(queries), grad_w)


def solution(mesh):
    return jax.shard_map(
        functools.partial(per_device, mesh.shape["blk"]),
        mesh=mesh,
        in_specs=(
            P(("groups", "blk"), None, None),
            P(("groups", "blk"), None, None),
            P(),
            P(("groups", "blk"), None),
            P(("groups", "blk")),
            P(("groups", "blk")),
            P(("groups", "blk")),
        ),
        out_specs=(P(("groups", "blk")), P(("groups", "blk"), None)),
        check_vma=False,
    )
```

```python
import functools

import jax
import jax.numpy as jnp
from jax import lax
from jax.experimental import pallas as pl
from jax.experimental.pallas import tpu as pltpu
from jax.sharding import PartitionSpec as P

CYCLE = 4
HEAT = 0.05
EPSILON = 1e-06
NT = (((1,), (1,)), ((), ()))
TN = (((0,), (0,)), ((), ()))


def dot32(a, b, dims):
    return lax.dot_general(
        a, b, dims, precision=lax.Precision.HIGHEST, preferred_element_type=jnp.float32
    )


def kernel(
    n, link_dtype,
    qh_ref, ph_ref, proj_ref, rows_ref, pos_ref, cnt_ref, len_ref,
    loss_ref, grad_ref,
    teach_own, teach_all, qraw, q_all, pv, plen, pu, put, exps, den, w_buf, pgrad,
    s_send, s_recv, g_send, g_recv, qg_send, qg_recv, part, part_own, part_recv,
    teach_ss, teach_rs, q_ss, q_rs, s_ss, s_rs, g_ss, g_rs, qg_ss, qg_rs, part_ss, part_rs,
):
    me = lax.axis_index("blk")
    queries, q_tokens, width = qh_ref.shape
    passages, p_tokens, _ = ph_ref.shape
    dim = proj_ref.shape[1]
    q_rows = queries * q_tokens
    padded = pu.shape[0] // passages

    def peer(shift):
        return lax.rem(me + shift + n, n)

    def remote(src, dst, ss, rs, target):
        return pltpu.make_async_remote_copy(
            src_ref=src, dst_ref=dst, send_sem=ss, recv_sem=rs,
            device_id={"blk": target}, device_id_type=pl.DeviceIdType.MESH,
        )

    barrier = pltpu.get_barrier_semaphore()

    @pl.loop(1, n)
    def _(k):
        pl.semaphore_signal(
            barrier, inc=1, device_id={"blk": peer(k)}, device_id_type=pl.DeviceIdType.MESH
        )

    projection = proj_ref[...]
    q_hidden = qh_ref[...].reshape(q_rows, width)
    raw = jnp.dot(q_hidden, projection, preferred_element_type=jnp.float32)
    qraw[...] = raw
    q_len = jnp.sqrt(jnp.sum(raw * raw, axis=1, keepdims=True) + EPSILON)
    q_all[0] = (raw / q_len).astype(jnp.bfloat16)
    teach_own[...] = jnp.zeros(teach_own.shape, jnp.float32)
    teach_own[:, : rows_ref.shape[1]] = rows_ref[...]
    teach_all[me] = teach_own[...]
    pl.semaphore_wait(barrier, n - 1)

    def q_copy(o):
        return remote(q_all.at[0], q_all.at[o], q_ss.at[o], q_rs.at[o], peer(o))

    for o in reversed(range(1, CYCLE)):
        q_copy(o).start()

    def teach_send(k):
        return remote(teach_own, teach_all.at[me], teach_ss.at[k], teach_rs.at[k], peer(k))

    def teach_recv(k):
        return remote(teach_own, teach_all.at[peer(-k)], teach_ss.at[k], teach_rs.at[k], peer(k))

    @pl.loop(1, n)
    def _(k):
        teach_send(k).start()

    pv[...] = jnp.zeros(pv.shape, jnp.float32)
    plen[...] = jnp.ones(plen.shape, jnp.float32)

    for p in range(passages):
        at = p * padded
        raw_p = jnp.dot(ph_ref[p], projection, preferred_element_type=jnp.float32)
        length = jnp.sqrt(jnp.sum(raw_p * raw_p, axis=1, keepdims=True) + EPSILON)
        pv[at : at + p_tokens] = raw_p / length
        plen[at : at + p_tokens] = jnp.broadcast_to(length, raw_p.shape)
    pu[...] = pv[...].astype(jnp.bfloat16)
    put[...] = jnp.transpose(pv[...]).astype(jnp.bfloat16)
    pgrad[...] = jnp.zeros(pgrad.shape, jnp.float32)

    low = lax.broadcasted_iota(jnp.int32, (queries, q_rows), 0) * q_tokens
    lane = lax.broadcasted_iota(jnp.int32, (queries, q_rows), 1)
    spread = jnp.where((lane >= low) & (lane < low + q_tokens), 1.0, 0.0)
    token = lax.broadcasted_iota(jnp.int32, (padded, q_rows), 0)

    s_send[...] = jnp.zeros(s_send.shape, jnp.float32)
    g_send[...] = jnp.zeros(g_send.shape, jnp.float32)

    def s_copy(o):
        return remote(s_send.at[o], s_recv.at[o], s_ss.at[o], s_rs.at[o], peer(-o))

    def g_copy(o):
        return remote(g_send.at[o], g_recv.at[o], g_ss.at[o], g_rs.at[o], peer(o))

    def qg_copy(o):
        return remote(qg_send.at[o], qg_recv.at[o], qg_ss.at[o], qg_rs.at[o], peer(-o))

    def score(o):
        units = q_all[o]

        @pl.loop(0, passages, unroll=8)
        def _(p):
            at = pl.ds(pl.multiple_of(p * padded, padded), padded)
            sims = lax.dot_general(pu[at], units, NT, preferred_element_type=jnp.float32)
            e = jnp.where(token < len_ref[0, p], jnp.exp(sims * (1.0 / HEAT)), 0.0)
            exps[o, at] = e
            den[o, pl.ds(p, 1)] = jnp.sum(e, axis=0, keepdims=True)

        peaks = HEAT * jnp.log(den[o])
        return dot32(peaks, spread, NT)

    own_scores = score(0)
    for o in range(1, CYCLE):
        q_copy(o).wait_recv()
        s_send[o, :, :queries] = score(o)
        s_copy(o).start()

    @pl.loop(1, n)
    def _(k):
        teach_recv(k).wait_recv()

    stored = teach_all[...].reshape(n * queries, teach_all.shape[2])
    cand = CYCLE * passages
    rows = lax.broadcasted_iota(jnp.int32, (n * queries, queries), 0)
    pick = jnp.where(rows == pos_ref[...], 1.0, 0.0)
    teacher = dot32(jnp.transpose(stored)[:cand], pick, (((1,), (0,)), ((), ())))
    valid = lax.broadcasted_iota(jnp.int32, (cand, queries), 0) < cnt_ref[...]
    teacher_exp = jnp.where(valid, jnp.exp(teacher), 0.0)
    teacher_total = jnp.sum(teacher_exp, axis=0, keepdims=True)
    teacher_prob = teacher_exp / teacher_total
    teacher_log = teacher - jnp.log(teacher_total)

    student_parts = [own_scores]
    for o in range(1, CYCLE):
        s_copy(o).wait_recv()
        student_parts.append(s_recv[o, :, :queries])
    student = jnp.concatenate(student_parts, axis=0)
    student_exp = jnp.where(valid, jnp.exp(student), 0.0)
    student_total = jnp.sum(student_exp, axis=0, keepdims=True)
    score_grad = student_exp / student_total - teacher_prob
    for o in range(1, CYCLE):
        g_send[o, :, :queries] = score_grad[o * passages : (o + 1) * passages]
        g_copy(o).start()
    gap = teacher_log - (student - jnp.log(student_total))
    loss_ref[...] = jnp.sum(jnp.where(valid, teacher_prob * gap, 0.0), axis=0, keepdims=True)

    def backward(o, grads):
        units = q_all[o]
        den[o] = dot32(grads, spread, (((1,), (0,)), ((), ()))) / den[o]

        @pl.loop(0, passages, unroll=8)
        def _(p):
            at = pl.ds(pl.multiple_of(p * padded, padded), padded)
            w = (exps[o, at] * den[o, pl.ds(p, 1)]).astype(jnp.bfloat16)
            w_buf[at] = w

        q_grad = jnp.dot(put[...], w_buf[...], preferred_element_type=jnp.float32)
        if o > 0:
            qg_send[o] = q_grad.astype(link_dtype)
            qg_copy(o).start()
        pgrad[...] += jnp.dot(w_buf[...], units, preferred_element_type=jnp.float32)
        return q_grad

    q_total = backward(0, score_grad[:passages])
    for o in reversed(range(1, CYCLE)):
        g_copy(o).wait_recv()
        backward(o, g_recv[o, :, :queries])

    term = jnp.zeros((dim, width), jnp.float32)
    for p in range(passages):
        at = p * padded
        v = pv[at : at + p_tokens]
        g = pgrad[at : at + p_tokens]
        raw_g = (g - v * jnp.sum(v * g, axis=1, keepdims=True)) / plen[at : at + p_tokens]
        term = term + lax.dot_general(
            raw_g.astype(jnp.bfloat16), ph_ref[p], TN, preferred_element_type=jnp.float32
        )

    for o in range(1, CYCLE):
        qg_copy(o).wait_recv()
        q_total = q_total + qg_recv[o].astype(jnp.float32)
    g = jnp.transpose(q_total)
    raw = qraw[...]
    q_len = jnp.sqrt(jnp.sum(raw * raw, axis=1, keepdims=True) + EPSILON)
    v = raw / q_len
    raw_g = (g - v * jnp.sum(v * g, axis=1, keepdims=True)) / q_len
    term = term + lax.dot_general(
        raw_g.astype(jnp.bfloat16), qh_ref[...].reshape(q_rows, width), TN,
        preferred_element_type=jnp.float32,
    )
    whole = jnp.transpose(term)
    chunk = grad_ref.shape[0]
    for k in range(n):
        piece = whole[k * chunk : (k + 1) * chunk]
        part_own[k] = piece
        part[k] = piece.astype(link_dtype)

    def part_copy(k):
        return remote(part.at[peer(k)], part_recv.at[k], part_ss.at[k], part_rs.at[k], peer(k))

    @pl.loop(1, n)
    def _(k):
        part_copy(k).start()

    grad_ref[...] = part_own[me]

    @pl.loop(1, n)
    def _(k):
        part_copy(k).wait_recv()
        grad_ref[...] += part_recv[k].astype(jnp.float32)

    for o in range(1, CYCLE):
        q_copy(o).wait_send()
        s_copy(o).wait_send()
        g_copy(o).wait_send()
        qg_copy(o).wait_send()

    @pl.loop(1, n)
    def _(k):
        teach_send(k).wait_send()
        part_copy(k).wait_send()


def per_device(
    n, query_hidden, passage_hidden, projection, teacher_rows, teacher_pos, neg_count, pass_len
):
    queries, q_tokens, width = query_hidden.shape
    passages, p_tokens, _ = passage_hidden.shape
    dim = projection.shape[1]
    q_rows = queries * q_tokens
    padded = -(-p_tokens // 16) * 16
    p_rows = passages * padded
    chunk = width // n
    link_dtype = jnp.bfloat16
    f32, bf16 = jnp.float32, jnp.bfloat16
    vmem = pl.BlockSpec(memory_space=pltpu.VMEM)
    smem = pl.BlockSpec(memory_space=pltpu.SMEM)
    dma = pltpu.SemaphoreType.DMA
    loss, grad_w = pl.pallas_call(
        functools.partial(kernel, n, link_dtype),
        out_shape=(
            jax.ShapeDtypeStruct((1, queries), f32),
            jax.ShapeDtypeStruct((chunk, dim), f32),
        ),
        in_specs=[vmem] * 6 + [smem],
        out_specs=(vmem, vmem),
        scratch_shapes=[
            pltpu.VMEM((queries, 128), f32),
            pltpu.VMEM((n, queries, 128), f32),
            pltpu.VMEM((q_rows, dim), f32),
            pltpu.VMEM((CYCLE, q_rows, dim), bf16),
            pltpu.VMEM((p_rows, dim), f32),
            pltpu.VMEM((p_rows, dim), f32),
            pltpu.VMEM((p_rows, dim), bf16),
            pltpu.VMEM((dim, p_rows), bf16),
            pltpu.VMEM((CYCLE, p_rows, q_rows), f32),
            pltpu.VMEM((CYCLE, passages, q_rows), f32),
            pltpu.VMEM((p_rows, q_rows), bf16),
            pltpu.VMEM((p_rows, dim), f32),
            pltpu.VMEM((CYCLE, passages, 128), f32),
            pltpu.VMEM((CYCLE, passages, 128), f32),
            pltpu.VMEM((CYCLE, passages, 128), f32),
            pltpu.VMEM((CYCLE, passages, 128), f32),
            pltpu.VMEM((CYCLE, dim, q_rows), link_dtype),
            pltpu.VMEM((CYCLE, dim, q_rows), link_dtype),
            pltpu.VMEM((n, chunk, dim), link_dtype),
            pltpu.VMEM((n, chunk, dim), f32),
            pltpu.VMEM((n, chunk, dim), link_dtype),
            dma((n,)), dma((n,)),
            dma((CYCLE,)), dma((CYCLE,)),
            dma((CYCLE,)), dma((CYCLE,)),
            dma((CYCLE,)), dma((CYCLE,)),
            dma((CYCLE,)), dma((CYCLE,)),
            dma((n,)), dma((n,)),
        ],
        compiler_params=pltpu.CompilerParams(
            collective_id=0, has_side_effects=True, vmem_limit_bytes=50 * 1024 * 1024
        ),
    )(
        query_hidden,
        passage_hidden,
        projection,
        teacher_rows,
        teacher_pos.reshape(1, queries),
        neg_count.reshape(1, queries),
        pass_len.reshape(1, passages),
    )
    return (loss.reshape(queries), grad_w)


def solution(mesh):
    return jax.shard_map(
        functools.partial(per_device, mesh.shape["blk"]),
        mesh=mesh,
        in_specs=(
            P(("groups", "blk"), None, None),
            P(("groups", "blk"), None, None),
            P(),
            P(("groups", "blk"), None),
            P(("groups", "blk")),
            P(("groups", "blk")),
            P(("groups", "blk")),
        ),
        out_specs=(P(("groups", "blk")), P(("groups", "blk"), None)),
        check_vma=False,
    )
```
